32 devices in a mesh: seq: 8 (over y, x, core), head: 4 (over z).
Axes of the slice: x: 2, y: 2, z: 4, core: 2. Of those that a mesh axis runs over, the one named last changes fastest.
Arguments:
- query_tokens: bfloat16 [5120, 3072], P(('seq', 'head')), may hold values from -6 to 6
- key_tokens: bfloat16 [5120, 3072], P(('seq', 'head')), may hold values from -6 to 6
- value_tokens: bfloat16 [5120, 3072], P(('seq', 'head')), may hold values from -6 to 6
- matching: int32 [2, 8], replicated, may hold values from 0 to 7, as said below
Outputs:
- attended: bfloat16 [5120, 3072], P(('seq', 'head'))
The draws below stay inside these ranges and needn't reach their ends.
Inputs may be any that keep to these rules, and one draw needn't show every extreme that they name: For each round r and block b: matching[r, matching[r, b]] == b and matching[r, b] != b; the 2 rows give every block different partners.
All inputs are finite; a program needn't handle non-finite values.
Results may differ from the reference program's by a relative error of at most 0.0048.
Values may be sent and summed in bfloat16 or wider, within the bound.
No kernel may reach another device: no remote copies, remote signals or barrier semaphores. Data moves between devices by JAX's collectives and lax.ppermute only.
A program may use at most 64 MiB of HBM per device.

```python
import jax
import jax.numpy as jnp
from jax import lax

HEADS = 24
HEAD_DIM = 128
WIDTH = 3072
ROUNDS = 2
BLOCKS = 8
BLOCK_TOK = 640
TOKENS = 5120


def drawn_pair(key):
    query_base = jnp.clip(jax.random.normal(jax.random.fold_in(key, 21), (TOKENS, WIDTH), jnp.float32), -6.0, 6.0)
    key_base = jnp.clip(jax.random.normal(jax.random.fold_in(key, 22), (TOKENS, WIDTH), jnp.float32), -6.0, 6.0)
    return (query_base, key_base)


def draw_query_tokens(key, part):
    return drawn_pair(jax.random.fold_in(key, 5))[0].astype(jnp.bfloat16)


def draw_key_tokens(key, part):
    return drawn_pair(jax.random.fold_in(key, 5))[1].astype(jnp.bfloat16)


def draw_matching(key, part):
    count = BLOCKS
    relabel = jax.random.permutation(jax.random.fold_in(key, 31), count).astype(jnp.int32)
    first_round = jax.random.randint(jax.random.fold_in(key, 32), (), 0, count - 1)
    second_round = (first_round + jax.random.randint(jax.random.fold_in(key, 33), (), 1, count - 1)) % (count - 1)
    players = jnp.arange(count, dtype=jnp.int32)

    def circle(turn):
        other = (2 * turn - players) % (count - 1)
        base = jnp.where(players == count - 1, turn, jnp.where(players == turn, count - 1, other))
        return jnp.zeros((count,), jnp.int32).at[relabel].set(relabel[base])
    return jnp.stack([circle(first_round), circle(second_round)]).astype(jnp.int32)


def levels(key, dims, pieces, least, top_value):
    gain = 1.0
    for position, parts in pieces:
        heights = jax.random.uniform(jax.random.fold_in(jax.random.fold_in(key, 6), position), (parts,), jnp.float32, least / len(pieces), top_value / len(pieces))
        gain = gain * jnp.repeat(jnp.exp(heights), dims[position] // parts).reshape((-1,) + (1,) * (len(dims) - 1 - position))
    return gain


def scatter_about(stream_key, extent, width, bound, split=(), kind=jnp.bfloat16):
    values = jax.random.normal(stream_key, extent, jnp.float32) * width
    if len(split) > 0:
        values = levels(stream_key, extent, split, -0.22, 0.18) * values
    return jnp.clip(values, min=-bound, max=bound).astype(kind)


def setup_inputs(seed: int = 0) -> dict:
    splits = jax.random.split(jax.random.key(seed), 5)
    return {
        "query_tokens": draw_query_tokens(jax.random.fold_in(splits[4], 71), 0),
        "key_tokens": draw_key_tokens(jax.random.fold_in(splits[4], 71), 0),
        "value_tokens": scatter_about(splits[2], (TOKENS, WIDTH), 1.0, 6.0, ((0, 32),)),
        "matching": draw_matching(jax.random.fold_in(splits[4], 71), 0),
    }


def reference(query_tokens, key_tokens, value_tokens, matching):
    query_blocks = query_tokens.reshape(BLOCKS, BLOCK_TOK, WIDTH)
    key_blocks = key_tokens.reshape(BLOCKS, BLOCK_TOK, WIDTH)
    value_blocks = value_tokens.reshape(BLOCKS, BLOCK_TOK, WIDTH)
    score_scale = 1.0 / (HEAD_DIM ** 0.5)

    def one_block(index):
        key_list = [key_blocks[index]]
        value_list = [value_blocks[index]]
        for round_index in range(ROUNDS):
            partner = matching[round_index, index]
            key_list.append(key_blocks[partner])
            value_list.append(value_blocks[partner])
        key_rows = jnp.concatenate(key_list, 0).astype(jnp.float32).reshape(-1, HEADS, HEAD_DIM)
        value_rows = jnp.concatenate(value_list, 0).astype(jnp.float32).reshape(-1, HEADS, HEAD_DIM)
        query_rows = query_blocks[index].astype(jnp.float32).reshape(BLOCK_TOK, HEADS, HEAD_DIM)
        scores = jnp.einsum("qhd,khd->hqk", query_rows, key_rows) * score_scale
        weights = jnp.exp(scores - jnp.max(scores, axis=-1, keepdims=True))
        totals = jnp.sum(weights, axis=-1)
        rounded = weights.astype(jnp.bfloat16).astype(jnp.float32)
        mixed = jnp.einsum("hqk,khd->qhd", rounded, value_rows)
        result = mixed / jnp.transpose(totals)[:, :, None]
        return result.reshape(BLOCK_TOK, WIDTH).astype(jnp.bfloat16)

    attended = lax.map(one_block, jnp.arange(BLOCKS, dtype=jnp.int32))
    return attended.reshape(TOKENS, WIDTH)
```

```python
import math

import jax
import jax.numpy as jnp
from jax import lax
from jax.experimental import pallas as pl
from jax.experimental.pallas import tpu as pltpu
from jax.sharding import PartitionSpec as P

HEAD_DIM = 128
ROUNDS = 2
CHUNKS = 3


def attend(query_rows, key_rows, value_rows, head_size):
    row_count, feature_width = query_rows.shape
    heads_here = feature_width // head_size
    block_rows = math.gcd(row_count, 512)
    score_scale = 1.0 / math.sqrt(head_size)
    key_heads = key_rows.reshape(-1, heads_here, head_size)
    value_heads = value_rows.reshape(-1, heads_here, head_size)
    query_blocks = query_rows.reshape(row_count // block_rows, block_rows, heads_here, head_size)

    def one_block(query_block):
        scores = (
            jnp.einsum("qhd,khd->hqk", query_block, key_heads, preferred_element_type=jnp.float32)
            * score_scale
        )
        weights = jnp.exp(scores - jnp.max(scores, axis=-1, keepdims=True))
        totals = jnp.sum(weights, axis=-1)
        mixed = jnp.einsum(
            "hqk,khd->qhd",
            weights.astype(jnp.bfloat16),
            value_heads,
            preferred_element_type=jnp.float32,
        )
        return (mixed / jnp.transpose(totals)[:, :, None]).astype(jnp.bfloat16)

    return lax.map(one_block, query_blocks).reshape(row_count, feature_width)


def routed(query_tokens, key_tokens, value_tokens, matching):
    seq_count = lax.axis_size("seq")
    local_query, local_keys, local_values = (
        lax.all_to_all(t, "head", split_axis=1, concat_axis=0, tiled=True)
        for t in (query_tokens, key_tokens, value_tokens)
    )
    block_count, feature_width = local_keys.shape
    piece_rows = block_count // seq_count

    def partners(local):
        spread = lax.all_to_all(
            local.reshape(seq_count, piece_rows, feature_width),
            "seq",
            split_axis=0,
            concat_axis=0,
            tiled=True,
        )
        found = lax.all_to_all(
            jnp.take(spread, matching, axis=0), "seq", split_axis=1, concat_axis=1, tiled=True
        )
        return found.reshape(ROUNDS * block_count, feature_width)

    key_rows = jnp.concatenate([local_keys, partners(local_keys)], 0)
    value_rows = jnp.concatenate([local_values, partners(local_values)], 0)
    attended = attend(local_query, key_rows, value_rows, HEAD_DIM)
    return lax.all_to_all(attended, "head", split_axis=0, concat_axis=1, tiled=True)


def split_kernel(count, columns, *refs):
    keys, values, outs = refs[:count], refs[count : 2 * count], refs[2 * count :]
    for d in range(count):
        outs[d][0] = keys[d][...]
        outs[d][1] = values[d][...]


def split_pairs(columns, key_tokens, value_tokens, width):
    count = columns.shape[0]
    rows = key_tokens.shape[0]
    specs = [pl.BlockSpec((rows, width), lambda i, c, d=d: (0, c[d])) for d in range(count)]
    return pl.pallas_call(
        lambda *refs: split_kernel(count, *refs),
        grid_spec=pltpu.PrefetchScalarGridSpec(
            num_scalar_prefetch=1,
            grid=(1,),
            in_specs=specs + specs,
            out_specs=[pl.BlockSpec((2, rows, width), lambda i, c: (0, 0, 0))] * count,
        ),
        out_shape=[jax.ShapeDtypeStruct((2, rows, width), key_tokens.dtype)] * count,
    )(columns, *([key_tokens] * count), *([value_tokens] * count))


def split_one(columns, tokens, width):
    count = columns.shape[0]
    rows = tokens.shape[0]

    def kernel(c, *refs):
        for d in range(count):
            refs[count + d][...] = refs[d][...]

    return pl.pallas_call(
        kernel,
        grid_spec=pltpu.PrefetchScalarGridSpec(
            num_scalar_prefetch=1,
            grid=(1,),
            in_specs=[pl.BlockSpec((rows, width), lambda i, c, d=d: (0, c[d])) for d in range(count)],
            out_specs=[pl.BlockSpec((rows, width), lambda i, c: (0, 0))] * count,
        ),
        out_shape=[jax.ShapeDtypeStruct((rows, width), tokens.dtype)] * count,
    )(columns, *([tokens] * count))


def pack(pieces):
    count = len(pieces)
    rows, width = pieces[0].shape[1:]

    def kernel(*refs):
        for d in range(count):
            refs[count][:, pl.ds(d * rows, rows), :] = refs[d][...]

    return pl.pallas_call(
        kernel,
        in_specs=[pl.BlockSpec(memory_space=pltpu.VMEM)] * count,
        out_specs=pl.BlockSpec(memory_space=pltpu.VMEM),
        out_shape=jax.ShapeDtypeStruct((2, count * rows, width), pieces[0].dtype),
    )(*pieces)


def pick(offsets, own, near, far, cross_keys, cross_values):
    def kernel(offs, own, near, far, cross_keys, cross_values, out):
        for r in range(ROUNDS):
            off = offs[r]

            @pl.when(off == 0)
            def _():
                out[r] = own[...]

            @pl.when(off == 2)
            def _():
                out[r] = near[...]

            @pl.when(off == 4)
            def _():
                out[r] = far[...]

            @pl.when(off == 6)
            def _():
                out[r, 0] = cross_keys[...]
                out[r, 1] = cross_values[...]

            @pl.when(off % 2 == 1)
            def _():
                out[r] = own[...]

    return pl.pallas_call(
        kernel,
        in_specs=[pl.BlockSpec(memory_space=pltpu.SMEM)] + [pl.BlockSpec(memory_space=pltpu.VMEM)] * 5,
        out_specs=pl.BlockSpec(memory_space=pltpu.VMEM),
        out_shape=jax.ShapeDtypeStruct((ROUNDS,) + own.shape, own.dtype),
    )(offsets, own, near, far, cross_keys, cross_values)


def attention_kernel(count, head_size, scale, offs, own, near, far, cross_keys, cross_values, paired, *refs):
    queries, outs = refs[:count], refs[count : 2 * count]
    keys, values = refs[2 * count :]
    block = own.shape[1]
    keys[pl.ds(0, block)] = own[0]
    values[pl.ds(0, block)] = own[1]
    for r in range(ROUNDS):
        off = offs[r]
        here = pl.ds((r + 1) * block, block)

        @pl.when(off == 2)
        def _():
            keys[here] = near[0]
            values[here] = near[1]

        @pl.when(off == 4)
        def _():
            keys[here] = far[0]
            values[here] = far[1]

        @pl.when(off == 6)
        def _():
            keys[here] = cross_keys[...]
            values[here] = cross_values[...]

        @pl.when(off % 2 == 1)
        def _():
            keys[here] = paired[r, 0]
            values[here] = paired[r, 1]

    for h in range(own.shape[2] // head_size):
        cols = slice(h * head_size, (h + 1) * head_size)
        for d in range(count):
            scores = lax.dot_general(
                queries[d][:, cols],
                keys[:, cols],
                (((1,), (1,)), ((), ())),
                preferred_element_type=jnp.float32,
            )
            top = jnp.max(scores, axis=1, keepdims=True)
            weights = jnp.exp2((scores - top) * scale)
            totals = jnp.sum(weights, axis=1, keepdims=True)
            mixed = jnp.dot(
                weights.astype(jnp.bfloat16), values[:, cols], preferred_element_type=jnp.float32
            )
            outs[d][:, cols] = (mixed / totals).astype(outs[d].dtype)


def attend_chunk(offsets, own, near, far, cross_keys, cross_values, paired, queries, chunk, head_size):
    count = len(queries)
    block, width = own.shape[1:]
    rows = queries[0].shape[0]
    scale = math.log2(math.e) / math.sqrt(head_size)
    whole = pl.BlockSpec(memory_space=pltpu.VMEM)
    flops = 4 * count * rows * (1 + ROUNDS) * block * width
    return pl.pallas_call(
        lambda *refs: attention_kernel(count, head_size, scale, *refs),
        grid=(1,),
        in_specs=[pl.BlockSpec(memory_space=pltpu.SMEM)]
        + [whole] * 6
        + [pl.BlockSpec((rows, width), lambda i: (0, chunk))] * count,
        out_specs=[pl.BlockSpec((rows, width), lambda i: (0, 0))] * count,
        out_shape=[jax.ShapeDtypeStruct((rows, width), own.dtype)] * count,
        scratch_shapes=[pltpu.VMEM(((1 + ROUNDS) * block, width), own.dtype)] * 2,
        cost_estimate=pl.CostEstimate(
            flops=flops, bytes_accessed=12 * block * width * 2, transcendentals=flops // (4 * head_size)
        ),
    )(offsets, own, near, far, cross_keys, cross_values, paired, *queries)


def join(columns, pieces, width, total):
    chunks, count = len(pieces), len(pieces[0])
    rows = pieces[0][0].shape[0]

    def kernel(c, *refs):
        out = refs[chunks * count]
        for d in range(count):
            for j in range(chunks):
                start = pl.multiple_of((c[d] + j) * width, width)
                out[:, pl.ds(start, width)] = refs[j * count + d][...]

    return pl.pallas_call(
        kernel,
        in_specs=[pl.BlockSpec(memory_space=pltpu.SMEM)]
        + [pl.BlockSpec(memory_space=pltpu.VMEM)] * (chunks * count),
        out_specs=pl.BlockSpec(memory_space=pltpu.VMEM),
        out_shape=jax.ShapeDtypeStruct((rows, total), pieces[0][0].dtype),
    )(columns, *[p for per in pieces for p in per])


def cube(query_tokens, key_tokens, value_tokens, matching):
    seq_count, head_count = lax.axis_size("seq"), lax.axis_size("head")
    me, place = lax.axis_index("seq"), lax.axis_index("head")
    rows, total = key_tokens.shape
    width = total // head_count // CHUNKS

    def over_seq(x, bits):
        return lax.ppermute(x, "seq", [(i, i ^ bits) for i in range(seq_count)])

    def over_head(x, bits):
        return lax.ppermute(x, "head", [(i, i ^ bits) for i in range(head_count)])

    ways = range(head_count)
    mates = jnp.bitwise_xor(place, jnp.arange(head_count, dtype=jnp.int32))
    columns = mates * CHUNKS
    mine = jnp.bitwise_xor(lax.dynamic_index_in_dim(matching, me, 1, False), me)
    other = jnp.bitwise_xor(me, 1)
    theirs = jnp.bitwise_xor(lax.dynamic_index_in_dim(matching, other, 1, False), me)

    stacked = []
    for j in range(CHUNKS):
        pieces = split_pairs(columns + j, key_tokens, value_tokens, width)
        stacked.append([pieces[0]] + [over_head(pieces[d], d) for d in ways if d])
    queries = split_one(mates, query_tokens, width * CHUNKS)
    queries = [queries[0]] + [over_head(queries[d], d) for d in ways if d]

    results = []
    for j in range(CHUNKS):
        own = pack(stacked[j])
        near, far = over_seq(own, 2), over_seq(own, 4)
        cross_keys = over_seq(near[0], 4)
        cross_values = over_seq(far[1], 2)
        paired = over_seq(pick(theirs, own, near, far, cross_keys, cross_values), 1)
        outs = attend_chunk(
            mine, own, near, far, cross_keys, cross_values, paired, queries, j, HEAD_DIM
        )
        results.append([outs[0]] + [over_head(outs[d], d) for d in ways if d])
    return join(columns, results, width, total)


def per_device(query_tokens, key_tokens, value_tokens, matching):
    seq_count, head_count = lax.axis_size("seq"), lax.axis_size("head")
    heads_here = key_tokens.shape[1] // HEAD_DIM // head_count
    small = seq_count == 2**3 and head_count & (head_count - 1) == 0
    if small and heads_here % CHUNKS == 0:
        return cube(query_tokens, key_tokens, value_tokens, matching)
    return routed(query_tokens, key_tokens, value_tokens, matching)


def solution(mesh):
    return jax.shard_map(
        per_device,
        mesh=mesh,
        in_specs=(
            P(("seq", "head"), None),
            P(("seq", "head"), None),
            P(("seq", "head"), None),
            P(),
        ),
        out_specs=P(("seq", "head"), None),
        check_vma=False,
    )
```

```python
import math

import jax
import jax.numpy as jnp
from jax import lax
from jax.experimental import pallas as pl
from jax.experimental.pallas import tpu as pltpu
from jax.sharding import PartitionSpec as P


HEAD_DIM = 128
ROUNDS = 2
CHUNKS = 3
TILE_PIECES = 2


def attend(query_rows, key_rows, value_rows, head_size):
    row_count, feature_width = query_rows.shape
    heads_here = feature_width // head_size
    block_rows = math.gcd(row_count, 512)
    score_scale = 1.0 / math.sqrt(head_size)
    key_heads = key_rows.reshape(-1, heads_here, head_size)
    value_heads = value_rows.reshape(-1, heads_here, head_size)
    query_blocks = query_rows.reshape(row_count // block_rows, block_rows, heads_here, head_size)

    def one_block(query_block):
        scores = (
            jnp.einsum("qhd,khd->hqk", query_block, key_heads, preferred_element_type=jnp.float32)
            * score_scale
        )
        weights = jnp.exp(scores - jnp.max(scores, axis=-1, keepdims=True))
        totals = jnp.sum(weights, axis=-1)
        mixed = jnp.einsum(
            "hqk,khd->qhd",
            weights.astype(jnp.bfloat16),
            value_heads,
            preferred_element_type=jnp.float32,
        )
        return (mixed / jnp.transpose(totals)[:, :, None]).astype(jnp.bfloat16)

    return lax.map(one_block, query_blocks).reshape(row_count, feature_width)


def routed(query_tokens, key_tokens, value_tokens, matching):
    seq_count = lax.axis_size("seq")
    local_query, local_keys, local_values = (
        lax.all_to_all(t, "head", split_axis=1, concat_axis=0, tiled=True)
        for t in (query_tokens, key_tokens, value_tokens)
    )
    block_count, feature_width = local_keys.shape
    piece_rows = block_count // seq_count

    def partners(local):
        spread = lax.all_to_all(
            local.reshape(seq_count, piece_rows, feature_width),
            "seq",
            split_axis=0,
            concat_axis=0,
            tiled=True,
        )
        found = lax.all_to_all(
            jnp.take(spread, matching, axis=0), "seq", split_axis=1, concat_axis=1, tiled=True
        )
        return found.reshape(ROUNDS * block_count, feature_width)

    key_rows = jnp.concatenate([local_keys, partners(local_keys)], 0)
    value_rows = jnp.concatenate([local_values, partners(local_values)], 0)
    attended = attend(local_query, key_rows, value_rows, HEAD_DIM)
    return lax.all_to_all(attended, "head", split_axis=0, concat_axis=1, tiled=True)


SMALL = pltpu.CompilerParams(vmem_limit_bytes=8 * 2**20)


def split_pairs(columns, key_tokens, value_tokens, width):
    count = columns.shape[0]
    rows = key_tokens.shape[0]
    specs = [pl.BlockSpec((rows, width), lambda i, c, d=d: (0, c[d])) for d in range(count)]

    def kernel(c, *refs):
        for d in range(count):
            refs[2 * count + d][0] = refs[d][...]
            refs[2 * count + d][1] = refs[count + d][...]

    return pl.pallas_call(
        kernel,
        grid_spec=pltpu.PrefetchScalarGridSpec(
            num_scalar_prefetch=1,
            grid=(1,),
            in_specs=specs + specs,
            out_specs=[pl.BlockSpec((2, rows, width), lambda i, c: (0, 0, 0))] * count,
        ),
        out_shape=[jax.ShapeDtypeStruct((2, rows, width), key_tokens.dtype)] * count,
        compiler_params=SMALL,
    )(columns, *([key_tokens] * count), *([value_tokens] * count))


def split_one(columns, tokens, width):
    count = columns.shape[0]
    rows = tokens.shape[0]

    def kernel(c, *refs):
        for d in range(count):
            refs[count + d][...] = refs[d][...]

    return pl.pallas_call(
        kernel,
        grid_spec=pltpu.PrefetchScalarGridSpec(
            num_scalar_prefetch=1,
            grid=(1,),
            in_specs=[pl.BlockSpec((rows, width), lambda i, c, d=d: (0, c[d])) for d in range(count)],
            out_specs=[pl.BlockSpec((rows, width), lambda i, c: (0, 0))] * count,
        ),
        out_shape=[jax.ShapeDtypeStruct((rows, width), tokens.dtype)] * count,
        compiler_params=SMALL,
    )(columns, *([tokens] * count))


def pack(pieces):
    count = len(pieces)
    rows, width = pieces[0].shape[1:]

    def kernel(*refs):
        for d in range(count):
            refs[count][:, pl.ds(d * rows, rows), :] = refs[d][...]

    return pl.pallas_call(
        kernel,
        in_specs=[pl.BlockSpec(memory_space=pltpu.VMEM)] * count,
        out_specs=pl.BlockSpec(memory_space=pltpu.VMEM),
        out_shape=jax.ShapeDtypeStruct((2, count * rows, width), pieces[0].dtype),
        compiler_params=SMALL,
    )(*pieces)


def group_specs(own, first, chunk):
    rows, width = first.shape[1], own.shape[2]
    pair = pl.BlockSpec((2, rows, width), lambda i: (0, 0, chunk))
    half = pl.BlockSpec((rows, width), lambda i: (0, chunk))
    rest = pl.BlockSpec(own.shape, lambda i: (0, 0, 0))
    rest_half = pl.BlockSpec(own.shape[1:], lambda i: (0, 0))
    return [pair] * 3 + [half] * 2 + [rest] * 3 + [rest_half] * 2


def fetch(off, group, put):
    own0, near0, far0, cross_keys0, cross_values0, own, near, far, cross_keys, cross_values = group

    def both(first, rest):
        for i in range(2):
            put(i, first[i], rest[i])

    pl.when(off == 0)(lambda: both(own0, own))
    pl.when(off == 2)(lambda: both(near0, near))
    pl.when(off == 4)(lambda: both(far0, far))

    @pl.when(off == 6)
    def _():
        put(0, cross_keys0[...], cross_keys[...])
        put(1, cross_values0[...], cross_values[...])


def pick(offsets, firsts, rests, chunk):
    rows, (_, rest, width) = firsts[0].shape[1], rests[0].shape

    def kernel(offs, *refs):
        group, out = refs[:10], refs[10]
        for r in range(ROUNDS):

            def put(i, first, rest, r=r):
                out[r, i, pl.ds(0, rows)] = first
                out[r, i, pl.ds(rows, rest.shape[0])] = rest

            off = offs[r]
            fetch(jnp.where(off % 2 == 1, 0, off), group, put)

    shape = (ROUNDS, 2, rows + rest, width)
    return pl.pallas_call(
        kernel,
        grid=(1,),
        in_specs=[pl.BlockSpec(memory_space=pltpu.SMEM)] + group_specs(rests[0], firsts[0], chunk),
        out_specs=pl.BlockSpec(shape, lambda i: (0, 0, 0, 0)),
        out_shape=jax.ShapeDtypeStruct(shape, rests[0].dtype),
        compiler_params=pltpu.CompilerParams(vmem_limit_bytes=12 * 2**20),
    )(offsets, *firsts, *rests)


def attention_kernel(count, head_size, scale, offs, *refs):
    group, paired, refs = refs[:10], refs[10], refs[11:]
    queries, outs = refs[:count], refs[count : 2 * count]
    keys, values, asked = refs[2 * count :]
    own0, own = group[0], group[5]
    rows, block = own0.shape[1], own0.shape[1] + own.shape[1]
    table = (keys, values)
    for i in range(2):
        table[i][pl.ds(0, rows)] = own0[i]
        table[i][pl.ds(rows, block - rows)] = own[i]
    for r in range(ROUNDS):
        start = (r + 1) * block

        def put(i, first, rest, start=start):
            table[i][pl.ds(start, rows)] = first
            table[i][pl.ds(start + rows, block - rows)] = rest

        off = offs[r]
        fetch(off, group, put)

        @pl.when(off % 2 == 1)
        def _():
            for i in range(2):
                table[i][pl.ds(start, block)] = paired[r, i]

    for d in range(count):
        asked[pl.ds(d * rows, rows)] = queries[d][...]
    group = TILE_PIECES
    for h in range(own.shape[2] // head_size):
        cols = slice(h * head_size, (h + 1) * head_size)
        for first in range(0, count, group):
            scores = lax.dot_general(
                asked[pl.ds(first * rows, group * rows), cols],
                keys[:, cols],
                (((1,), (1,)), ((), ())),
                preferred_element_type=jnp.float32,
            )
            top = jnp.max(scores, axis=1, keepdims=True)
            weights = jnp.exp2((scores - top) * scale)
            totals = jnp.sum(weights, axis=1, keepdims=True)
            mixed = jnp.dot(
                weights.astype(jnp.bfloat16), values[:, cols], preferred_element_type=jnp.float32
            )
            result = (mixed / totals).astype(outs[0].dtype)
            for d in range(group):
                outs[first + d][:, cols] = result[d * rows : (d + 1) * rows]


def attend_chunk(offsets, firsts, rests, paired, queries, chunk, head_size):
    count = len(queries)
    block, width = paired.shape[2:]
    rows = queries[0].shape[0]
    scale = math.log2(math.e) / math.sqrt(head_size)
    flops = 4 * count * rows * (1 + ROUNDS) * block * width
    return pl.pallas_call(
        lambda *refs: attention_kernel(count, head_size, scale, *refs),
        grid=(1,),
        in_specs=[pl.BlockSpec(memory_space=pltpu.SMEM)]
        + group_specs(rests[0], firsts[0], chunk)
        + [pl.BlockSpec(paired.shape, lambda i: (0, 0, 0, 0))]
        + [pl.BlockSpec((rows, width), lambda i: (0, chunk))] * count,
        out_specs=[pl.BlockSpec((rows, width), lambda i: (0, 0))] * count,
        out_shape=[jax.ShapeDtypeStruct((rows, width), paired.dtype)] * count,
        scratch_shapes=[pltpu.VMEM(((1 + ROUNDS) * block, width), paired.dtype)] * 2
        + [pltpu.VMEM((count * rows, width), paired.dtype)],
        cost_estimate=pl.CostEstimate(
            flops=flops, bytes_accessed=12 * block * width * 2, transcendentals=flops // (4 * head_size)
        ),
        compiler_params=pltpu.CompilerParams(vmem_limit_bytes=20 * 2**20),
    )(offsets, *firsts, *rests, paired, *queries)


def join(columns, pieces, width, total):
    chunks, count = len(pieces), len(pieces[0])
    rows = pieces[0][0].shape[0]

    def kernel(c, *refs):
        out = refs[chunks * count]
        for d in range(count):
            for j in range(chunks):
                start = pl.multiple_of((c[d] + j) * width, width)
                out[:, pl.ds(start, width)] = refs[j * count + d][...]

    return pl.pallas_call(
        kernel,
        in_specs=[pl.BlockSpec(memory_space=pltpu.SMEM)]
        + [pl.BlockSpec(memory_space=pltpu.VMEM)] * (chunks * count),
        out_specs=pl.BlockSpec(memory_space=pltpu.VMEM),
        out_shape=jax.ShapeDtypeStruct((rows, total), pieces[0][0].dtype),
        compiler_params=SMALL,
    )(columns, *[p for per in pieces for p in per])


def cube(query_tokens, key_tokens, value_tokens, matching):
    seq_count, head_count = lax.axis_size("seq"), lax.axis_size("head")
    me, place = lax.axis_index("seq"), lax.axis_index("head")
    _, total = key_tokens.shape
    width = total // head_count // CHUNKS

    def over_seq(x, bits):
        return lax.ppermute(x, "seq", [(i, i ^ bits) for i in range(seq_count)])

    def over_head(x, bits):
        return lax.ppermute(x, "head", [(i, i ^ bits) for i in range(head_count)])

    ways = range(head_count)
    mates = jnp.bitwise_xor(place, jnp.arange(head_count, dtype=jnp.int32))
    columns = mates * CHUNKS
    mine = jnp.bitwise_xor(lax.dynamic_index_in_dim(matching, me, 1, False), me)
    other = jnp.bitwise_xor(me, 1)
    theirs = jnp.bitwise_xor(lax.dynamic_index_in_dim(matching, other, 1, False), me)

    def spread(own):
        near, far = over_seq(own, 2), over_seq(own, 4)
        return own, near, far, over_seq(near[0], 4), over_seq(far[1], 2)

    (first,) = split_pairs(mates[:1], key_tokens, value_tokens, width * CHUNKS)
    firsts = spread(first)
    moved = []
    for j in range(CHUNKS):
        pieces = split_pairs(columns[1:] + j, key_tokens, value_tokens, width)
        moved.append([over_head(p, d) for d, p in zip(ways[1:], pieces)])
    queries = split_one(mates, query_tokens, width * CHUNKS)
    queries = [queries[0]] + [over_head(queries[d], d) for d in ways[1:]]

    results = []
    for j in range(CHUNKS):
        own = pack(moved[j])
        rests = spread(own)
        picked = pick(theirs, firsts, rests, j)
        paired = over_seq(picked, 1)
        outs = attend_chunk(mine, firsts, rests, paired, queries, j, HEAD_DIM)
        results.append([outs[0]] + [over_head(outs[d], d) for d in ways if d])
    return join(columns, results, width, total)


def fits_cube(seq_count, head_count, heads):
    power = head_count & (head_count - 1) == 0
    return seq_count == 2**3 and power and heads % (head_count * CHUNKS) == 0


def per_device(query_tokens, key_tokens, value_tokens, matching):
    seq_count, head_count = lax.axis_size("seq"), lax.axis_size("head")
    if fits_cube(seq_count, head_count, key_tokens.shape[1] // HEAD_DIM):
        return cube(query_tokens, key_tokens, value_tokens, matching)
    return routed(query_tokens, key_tokens, value_tokens, matching)


def solution(mesh):
    return jax.shard_map(
        per_device,
        mesh=mesh,
        in_specs=(
            P(("seq", "head"), None),
            P(("seq", "head"), None),
            P(("seq", "head"), None),
            P(),
        ),
        out_specs=P(("seq", "head"), None),
        check_vma=False,
    )
```

```python
import math

import jax
import jax.numpy as jnp
from jax import lax
from jax.experimental import pallas as pl
from jax.experimental.pallas import tpu as pltpu
from jax.sharding import PartitionSpec as P


HEAD_DIM = 128
ROUNDS = 2
SIXTHS = (2, 2, 2)
STAGES = (("k0", "v0"), ("k1", "v1"), ("k2", "v2"), ("q0",), ("q1", "q2"))
TILE_PIECES = 2
TILE_KEYS = 384
LANES = 128


def attend(query_rows, key_rows, value_rows, head_size):
    row_count, feature_width = query_rows.shape
    heads_here = feature_width // head_size
    block_rows = math.gcd(row_count, 512)
    score_scale = 1.0 / math.sqrt(head_size)
    key_heads = key_rows.reshape(-1, heads_here, head_size)
    value_heads = value_rows.reshape(-1, heads_here, head_size)
    query_blocks = query_rows.reshape(row_count // block_rows, block_rows, heads_here, head_size)

    def one_block(query_block):
        scores = (
            jnp.einsum("qhd,khd->hqk", query_block, key_heads, preferred_element_type=jnp.float32)
            * score_scale
        )
        weights = jnp.exp(scores - jnp.max(scores, axis=-1, keepdims=True))
        totals = jnp.sum(weights, axis=-1)
        mixed = jnp.einsum(
            "hqk,khd->qhd",
            weights.astype(jnp.bfloat16),
            value_heads,
            preferred_element_type=jnp.float32,
        )
        return (mixed / jnp.transpose(totals)[:, :, None]).astype(jnp.bfloat16)

    return lax.map(one_block, query_blocks).reshape(row_count, feature_width)


def routed(query_tokens, key_tokens, value_tokens, matching):
    seq_count = lax.axis_size("seq")
    local_query, local_keys, local_values = (
        lax.all_to_all(t, "head", split_axis=1, concat_axis=0, tiled=True)
        for t in (query_tokens, key_tokens, value_tokens)
    )
    block_count, feature_width = local_keys.shape
    piece_rows = block_count // seq_count

    def partners(local):
        spread = lax.all_to_all(
            local.reshape(seq_count, piece_rows, feature_width),
            "seq",
            split_axis=0,
            concat_axis=0,
            tiled=True,
        )
        found = lax.all_to_all(
            jnp.take(spread, matching, axis=0), "seq", split_axis=1, concat_axis=1, tiled=True
        )
        return found.reshape(ROUNDS * block_count, feature_width)

    key_rows = jnp.concatenate([local_keys, partners(local_keys)], 0)
    value_rows = jnp.concatenate([local_values, partners(local_values)], 0)
    attended = attend(local_query, key_rows, value_rows, HEAD_DIM)
    return lax.all_to_all(attended, "head", split_axis=0, concat_axis=1, tiled=True)


SCALARS = pl.BlockSpec(memory_space=pltpu.SMEM)
LOCAL = pl.BlockSpec(memory_space=pltpu.VMEM)


def local_call(kernel, shapes, scalars, arrays, grant=12, **options):
    return pl.pallas_call(
        kernel,
        in_specs=[SCALARS] * len(scalars) + [LOCAL] * len(arrays),
        out_specs=jax.tree.map(lambda _: LOCAL, shapes),
        out_shape=shapes,
        compiler_params=pltpu.CompilerParams(vmem_limit_bytes=grant * 2**20),
        **options,
    )(*scalars, *arrays)


def columns_of(bits, share, start, width):
    place = jnp.bitwise_xor(lax.axis_index("head"), bits)
    return pl.ds(pl.multiple_of(place * share + start, HEAD_DIM), width)


def partner_offsets(matching, flip):
    me = lax.axis_index("seq")
    return [
        jnp.bitwise_xor(matching[r, jnp.bitwise_xor(me, flip)], me) for r in range(ROUNDS)
    ]


def split(ways, parts):
    arrays = [array for array, *_ in parts]
    rows, total = arrays[0].shape[0], sum(width for *_, width in parts)

    def kernel(*refs):
        for d, out in zip(ways, refs[len(parts) :]):
            column = 0
            for ref, (_, share, start, width) in zip(refs, parts):
                out[:, column : column + width] = ref[:, columns_of(d, share, start, width)]
                column += width

    shape = jax.ShapeDtypeStruct((rows, total), arrays[0].dtype)
    return local_call(kernel, [shape] * len(ways), [], arrays)


def split_own(keys, values, queries, share):
    rows, dtype = keys.shape[0], keys.dtype

    def kernel(keys, values, queries, pair, asked):
        cols = columns_of(0, share, 0, share)
        pair[0], pair[1], asked[...] = keys[:, cols], values[:, cols], queries[:, cols]

    shapes = [
        jax.ShapeDtypeStruct((2, rows, share), dtype),
        jax.ShapeDtypeStruct((rows, share), dtype),
    ]
    return local_call(kernel, shapes, [], [keys, values, queries])


def pack(pieces, columns, width):
    count, rows = len(pieces), pieces[0].shape[0]

    def kernel(*refs):
        for d in range(count):
            for i in range(2):
                cols = slice(columns[i], columns[i] + width)
                refs[count][i, pl.ds(d * rows, rows)] = refs[d][:, cols]

    shape = jax.ShapeDtypeStruct((2, count * rows, width), pieces[0].dtype)
    return local_call(kernel, shape, [], pieces)


def halves(near, far):
    def kernel(near, far, keys, values):
        keys[...] = near[0]
        values[...] = far[1]

    shape = jax.ShapeDtypeStruct(near.shape[1:], near.dtype)
    return local_call(kernel, [shape, shape], [], [near, far])


def fetch(off, group, cols, put):
    own0, near0, far0, cross_keys0, cross_values0, own, near, far, cross_keys, cross_values = group

    def both(first, rest):
        for i in range(2):
            put(i, first[i, :, cols], rest[i])

    pl.when(off == 0)(lambda: both(own0, own))
    pl.when(off == 2)(lambda: both(near0, near))
    pl.when(off == 4)(lambda: both(far0, far))

    @pl.when(off == 6)
    def _():
        put(0, cross_keys0[:, cols], cross_keys[...])
        put(1, cross_values0[:, cols], cross_values[...])


def pick(matching, firsts, rests, start):
    rows, (_, rest, width) = firsts[0].shape[1], rests[0].shape

    def kernel(matching, *refs):
        group, out = refs[:10], refs[10]
        for r, off in enumerate(partner_offsets(matching, 1)):

            def put(i, first, rest, r=r):
                out[r, i, pl.ds(0, rows)] = first
                out[r, i, pl.ds(rows, rest.shape[0])] = rest

            fetch(jnp.where(off % 2 == 1, 0, off), group, slice(start, start + width), put)

    shape = jax.ShapeDtypeStruct((ROUNDS, 2, rows + rest, width), rests[0].dtype)
    return local_call(kernel, shape, [matching], [*firsts, *rests])


def fold(op, tile, total):
    for start in range(0, tile.shape[1], LANES):
        group = tile[:, start : start + LANES]
        total = group if total is None else op(total, group)
    return total


def attention_kernel(head_size, scale, first_column, asked_columns, matching, *refs):
    count = len(asked_columns)
    group, paired, refs = refs[:10], refs[10], refs[11:]
    queries, outs = refs[:count], refs[count : 2 * count]
    keys, values, asked, scores = refs[2 * count :]
    own0, own = group[0], group[5]
    picked = slice(first_column, first_column + own.shape[2])
    rows, block = own0.shape[1], own0.shape[1] + own.shape[1]
    table = (keys, values)
    for i in range(2):
        table[i][pl.ds(0, rows)] = own0[i, :, picked]
        table[i][pl.ds(rows, block - rows)] = own[i]
    for r, off in enumerate(partner_offsets(matching, 0)):
        start = (r + 1) * block

        def put(i, first, rest, start=start):
            table[i][pl.ds(start, rows)] = first
            table[i][pl.ds(start + rows, block - rows)] = rest

        fetch(off, group, picked, put)

        @pl.when(off % 2 == 1)
        def _():
            for i in range(2):
                table[i][pl.ds(start, block)] = paired[r, i]

    for d in range(count):
        here = slice(asked_columns[d], asked_columns[d] + own.shape[2])
        asked[pl.ds(d * rows, rows)] = queries[d][:, here]
    items = [
        (slice(h * head_size, (h + 1) * head_size), first)
        for h in range(own.shape[2] // head_size)
        for first in range(0, count, TILE_PIECES)
    ]
    height = TILE_PIECES * rows
    total = keys.shape[0]
    step = TILE_KEYS if total % TILE_KEYS == 0 else LANES
    tops = {}
    for i in range(len(items) + 1):
        best = sums = mixed = None
        if i > 0:
            top = jnp.max(tops[i - 1], axis=1, keepdims=True)
        for start in range(0, total, step):
            here = slice(start, start + step)
            if i < len(items):
                cols, first = items[i]
                found = lax.dot_general(
                    asked[first * rows : first * rows + height, cols],
                    keys[here, cols],
                    (((1,), (1,)), ((), ())),
                    preferred_element_type=jnp.float32,
                )
                scores[i % 2, :, here] = found
                best = fold(jnp.maximum, found, best)
            if i > 0:
                cols, first = items[i - 1]
                weights = jnp.exp2((scores[(i - 1) % 2, :, here] - top) * scale)
                sums = fold(jnp.add, weights, sums)
                part = jnp.dot(
                    weights.astype(jnp.bfloat16),
                    values[here, cols],
                    preferred_element_type=jnp.float32,
                )
                mixed = part if mixed is None else mixed + part
        tops[i] = best
        if i > 0:
            result = (mixed / jnp.sum(sums, axis=1, keepdims=True)).astype(outs[0].dtype)
            for d in range(TILE_PIECES):
                outs[first + d][:, cols] = result[d * rows : (d + 1) * rows]


def attend_chunk(matching, firsts, rests, paired, queries, asked_columns, head_size):
    count, rows = len(queries), queries[0].shape[0]
    block, width = paired.shape[2:]
    scale = math.log2(math.e) / math.sqrt(head_size)
    flops = 4 * count * rows * (1 + ROUNDS) * block * width
    shape = jax.ShapeDtypeStruct((rows, width), paired.dtype)
    return local_call(
        lambda *refs: attention_kernel(head_size, scale, asked_columns[0], asked_columns, *refs),
        [shape] * count,
        [matching],
        [*firsts, *rests, paired, *queries],
        grant=24,
        scratch_shapes=[pltpu.VMEM(((1 + ROUNDS) * block, width), paired.dtype)] * 2
        + [
            pltpu.VMEM((count * rows, width), paired.dtype),
            pltpu.VMEM((2, TILE_PIECES * rows, (1 + ROUNDS) * block), jnp.float32),
        ],
        cost_estimate=pl.CostEstimate(
            flops=flops, bytes_accessed=12 * block * width * 2, transcendentals=flops // (4 * head_size)
        ),
    )


def join(pieces, starts, total):
    chunks, count = len(pieces), len(pieces[0])
    share = total // count

    def kernel(*refs):
        for d in range(count):
            for j in range(chunks):
                cols = columns_of(d, share, starts[j], pieces[j][d].shape[1])
                refs[chunks * count][:, cols] = refs[j * count + d][...]

    shape = jax.ShapeDtypeStruct((pieces[0][0].shape[0], total), pieces[0][0].dtype)
    return local_call(kernel, shape, [], [p for per in pieces for p in per])


def cube(query_tokens, key_tokens, value_tokens, matching):
    seq_count, head_count = lax.axis_size("seq"), lax.axis_size("head")
    _, total = key_tokens.shape
    share = total // head_count
    widths = [share // 6 * size for size in SIXTHS]
    starts = [sum(widths[:j]) for j in range(len(SIXTHS))]
    chunks = range(len(SIXTHS))

    def over_seq(x, bits):
        return lax.ppermute(x, "seq", [(i, i ^ bits) for i in range(seq_count)])

    def exchange(x, bits):
        return lax.ppermute(x, "head", [(i, i ^ bits) for i in range(head_count)])

    ways = range(head_count)

    def spread(own):
        near, far = over_seq(own, 2), over_seq(own, 4)
        keys, values = halves(near, far)
        return own, near, far, over_seq(keys, 4), over_seq(values, 2)

    first, own_queries = split_own(key_tokens, value_tokens, query_tokens, share)
    firsts = spread(first)
    tokens = {"k": key_tokens, "v": value_tokens, "q": query_tokens}
    found = {}
    for stage in STAGES:
        which = [(name[0], int(name[1:])) for name in stage]
        parts = [(tokens[kind], share, starts[j], widths[j]) for kind, j in which]
        pieces = split(ways[1:], parts)
        pieces = [exchange(p, d) for d, p in zip(ways[1:], pieces)]
        column = 0
        for kind, j in which:
            found[kind, j] = pieces, column
            column += widths[j]

    results = []
    for j in chunks:
        pieces, column = found["k", j]
        own = pack(pieces, (column, found["v", j][1]), widths[j])
        rests = spread(own)
        picked = pick(matching, firsts, rests, starts[j])
        paired = over_seq(picked, 1)
        pieces, column = found["q", j]
        queries = [own_queries, *pieces]
        columns = [starts[j]] + [column] * len(pieces)
        outs = attend_chunk(matching, firsts, rests, paired, queries, columns, HEAD_DIM)
        results.append([outs[0]] + [exchange(outs[d], d) for d in ways[1:]])
    return join(results, starts, total)


def fits_cube(seq_count, head_count, heads):
    power = head_count & (head_count - 1) == 0
    return seq_count == 2**3 and power and heads % (head_count * 6) == 0


def per_device(query_tokens, key_tokens, value_tokens, matching):
    seq_count, head_count = lax.axis_size("seq"), lax.axis_size("head")
    if fits_cube(seq_count, head_count, key_tokens.shape[1] // HEAD_DIM):
        return cube(query_tokens, key_tokens, value_tokens, matching)
    return routed(query_tokens, key_tokens, value_tokens, matching)


def solution(mesh):
    return jax.shard_map(
        per_device,
        mesh=mesh,
        in_specs=(
            P(("seq", "head"), None),
            P(("seq", "head"), None),
            P(("seq", "head"), None),
            P(),
        ),
        out_specs=P(("seq", "head"), None),
        check_vma=False,
    )
```

```python
import math

import jax
import jax.numpy as jnp
from jax import lax
from jax.experimental import pallas as pl
from jax.experimental.pallas import tpu as pltpu
from jax.sharding import PartitionSpec as P


HEAD_DIM = 128
ROUNDS = 2
SIXTHS = (2, 2, 2)
STAGES = (("k0", "v0"), ("k1", "v1"), ("k2", "v2"), ("q0",), ("q1", "q2"))
TILE_PIECES = 2
TILE_KEYS = 384
LANES = 128


def attend(query_rows, key_rows, value_rows, head_size):
    row_count, feature_width = query_rows.shape
    heads_here = feature_width // head_size
    block_rows = math.gcd(row_count, 512)
    score_scale = 1.0 / math.sqrt(head_size)
    key_heads = key_rows.reshape(-1, heads_here, head_size)
    value_heads = value_rows.reshape(-1, heads_here, head_size)
    query_blocks = query_rows.reshape(row_count // block_rows, block_rows, heads_here, head_size)

    def one_block(query_block):
        scores = (
            jnp.einsum("qhd,khd->hqk", query_block, key_heads, preferred_element_type=jnp.float32)
            * score_scale
        )
        weights = jnp.exp(scores - jnp.max(scores, axis=-1, keepdims=True))
        totals = jnp.sum(weights, axis=-1)
        mixed = jnp.einsum(
            "hqk,khd->qhd",
            weights.astype(jnp.bfloat16),
            value_heads,
            preferred_element_type=jnp.float32,
        )
        return (mixed / jnp.transpose(totals)[:, :, None]).astype(jnp.bfloat16)

    return lax.map(one_block, query_blocks).reshape(row_count, feature_width)


def routed(query_tokens, key_tokens, value_tokens, matching):
    seq_count = lax.axis_size("seq")
    local_query, local_keys, local_values = (
        lax.all_to_all(t, "head", split_axis=1, concat_axis=0, tiled=True)
        for t in (query_tokens, key_tokens, value_tokens)
    )
    block_count, feature_width = local_keys.shape
    piece_rows = block_count // seq_count

    def partners(local):
        spread = lax.all_to_all(
            local.reshape(seq_count, piece_rows, feature_width),
            "seq",
            split_axis=0,
            concat_axis=0,
            tiled=True,
        )
        found = lax.all_to_all(
            jnp.take(spread, matching, axis=0), "seq", split_axis=1, concat_axis=1, tiled=True
        )
        return found.reshape(ROUNDS * block_count, feature_width)

    key_rows = jnp.concatenate([local_keys, partners(local_keys)], 0)
    value_rows = jnp.concatenate([local_values, partners(local_values)], 0)
    attended = attend(local_query, key_rows, value_rows, HEAD_DIM)
    return lax.all_to_all(attended, "head", split_axis=0, concat_axis=1, tiled=True)


SCALARS = pl.BlockSpec(memory_space=pltpu.SMEM)
LOCAL = pl.BlockSpec(memory_space=pltpu.VMEM)


def local_call(kernel, shapes, scalars, arrays, grant=12, **options):
    return pl.pallas_call(
        kernel,
        in_specs=[SCALARS] * len(scalars) + [LOCAL] * len(arrays),
        out_specs=jax.tree.map(lambda _: LOCAL, shapes),
        out_shape=shapes,
        compiler_params=pltpu.CompilerParams(vmem_limit_bytes=grant * 2**20),
        **options,
    )(*scalars, *arrays)


def columns_of(bits, share, start, width):
    place = jnp.bitwise_xor(lax.axis_index("head"), bits)
    return pl.ds(pl.multiple_of(place * share + start, HEAD_DIM), width)


def partner_offsets(matching, flip):
    me = lax.axis_index("seq")
    return [
        jnp.bitwise_xor(matching[r, jnp.bitwise_xor(me, flip)], me) for r in range(ROUNDS)
    ]


def split(ways, parts):
    arrays = [array for array, *_ in parts]
    rows, total = arrays[0].shape[0], sum(width for *_, width in parts)

    def kernel(*refs):
        for d, out in zip(ways, refs[len(parts) :]):
            column = 0
            for ref, (_, share, start, width) in zip(refs, parts):
                out[:, column : column + width] = ref[:, columns_of(d, share, start, width)]
                column += width

    shape = jax.ShapeDtypeStruct((rows, total), arrays[0].dtype)
    return local_call(kernel, [shape] * len(ways), [], arrays)


def split_own(keys, values, queries, share):
    rows, dtype = keys.shape[0], keys.dtype

    def kernel(keys, values, queries, pair, asked):
        cols = columns_of(0, share, 0, share)
        pair[0], pair[1], asked[...] = keys[:, cols], values[:, cols], queries[:, cols]

    shapes = [
        jax.ShapeDtypeStruct((2, rows, share), dtype),
        jax.ShapeDtypeStruct((rows, share), dtype),
    ]
    return local_call(kernel, shapes, [], [keys, values, queries])


def pack(pieces, columns, width):
    count, rows = len(pieces), pieces[0].shape[0]

    def kernel(*refs):
        for d in range(count):
            for i in range(2):
                cols = slice(columns[i], columns[i] + width)
                refs[count][i, pl.ds(d * rows, rows)] = refs[d][:, cols]

    shape = jax.ShapeDtypeStruct((2, count * rows, width), pieces[0].dtype)
    return local_call(kernel, shape, [], pieces)


def halves(near, far):
    def kernel(near, far, keys, values):
        keys[...] = near[0]
        values[...] = far[1]

    shape = jax.ShapeDtypeStruct(near.shape[1:], near.dtype)
    return local_call(kernel, [shape, shape], [], [near, far])


def fetch(off, group, cols, put):
    own0, near0, far0, cross_keys0, cross_values0, own, near, far, cross_keys, cross_values = group

    def both(first, rest):
        for i in range(2):
            put(i, first[i, :, cols], rest[i])

    pl.when(off == 0)(lambda: both(own0, own))
    pl.when(off == 2)(lambda: both(near0, near))
    pl.when(off == 4)(lambda: both(far0, far))

    @pl.when(off == 6)
    def _():
        put(0, cross_keys0[:, cols], cross_keys[...])
        put(1, cross_values0[:, cols], cross_values[...])


def pick(matching, firsts, rests, start):
    rows, (_, rest, width) = firsts[0].shape[1], rests[0].shape

    def kernel(matching, *refs):
        group, out = refs[:10], refs[10]
        for r, off in enumerate(partner_offsets(matching, 1)):

            def put(i, first, rest, r=r):
                out[r, i, pl.ds(0, rows)] = first
                out[r, i, pl.ds(rows, rest.shape[0])] = rest

            fetch(jnp.where(off % 2 == 1, 0, off), group, slice(start, start + width), put)

    shape = jax.ShapeDtypeStruct((ROUNDS, 2, rows + rest, width), rests[0].dtype)
    return local_call(kernel, shape, [matching], [*firsts, *rests])


def fold(op, tile, total):
    for start in range(0, tile.shape[1], LANES):
        group = tile[:, start : start + LANES]
        total = group if total is None else op(total, group)
    return total


def attention_kernel(head_size, scale, first_column, asked_columns, matching, *refs):
    count = len(asked_columns)
    group, paired, refs = refs[:10], refs[10], refs[11:]
    queries, outs = refs[:count], refs[count : 2 * count]
    keys, values, asked, scores = refs[2 * count :]
    own0, own = group[0], group[5]
    picked = slice(first_column, first_column + own.shape[2])
    rows, block = own0.shape[1], own0.shape[1] + own.shape[1]
    table = (keys, values)
    for i in range(2):
        table[i][pl.ds(0, rows)] = own0[i, :, picked]
        table[i][pl.ds(rows, block - rows)] = own[i]
    for r, off in enumerate(partner_offsets(matching, 0)):
        start = (r + 1) * block

        def put(i, first, rest, start=start):
            table[i][pl.ds(start, rows)] = first
            table[i][pl.ds(start + rows, block - rows)] = rest

        fetch(off, group, picked, put)

        @pl.when(off % 2 == 1)
        def _():
            for i in range(2):
                table[i][pl.ds(start, block)] = paired[r, i]

    for d in range(count):
        here = slice(asked_columns[d], asked_columns[d] + own.shape[2])
        asked[pl.ds(d * rows, rows)] = queries[d][:, here]
    items = [
        (slice(h * head_size, (h + 1) * head_size), first)
        for h in range(own.shape[2] // head_size)
        for first in range(0, count, TILE_PIECES)
    ]
    height = TILE_PIECES * rows
    total = keys.shape[0]
    step = TILE_KEYS if total % TILE_KEYS == 0 else LANES
    tops = {}
    for i in range(len(items) + 1):
        best = sums = mixed = None
        if i > 0:
            top = jnp.max(tops[i - 1], axis=1, keepdims=True)
        for start in range(0, total, step):
            here = slice(start, start + step)
            if i < len(items):
                cols, first = items[i]
                found = lax.dot_general(
                    asked[first * rows : first * rows + height, cols],
                    keys[here, cols],
                    (((1,), (1,)), ((), ())),
                    preferred_element_type=jnp.float32,
                )
                scores[i % 2, :, here] = found
                best = fold(jnp.maximum, found, best)
            if i > 0:
                cols, first = items[i - 1]
                weights = jnp.exp2((scores[(i - 1) % 2, :, here] - top) * scale)
                sums = fold(jnp.add, weights, sums)
                part = jnp.dot(
                    weights.astype(jnp.bfloat16),
                    values[here, cols],
                    preferred_element_type=jnp.float32,
                )
                mixed = part if mixed is None else mixed + part
        tops[i] = best
        if i > 0:
            result = (mixed / jnp.sum(sums, axis=1, keepdims=True)).astype(outs[0].dtype)
            for d in range(TILE_PIECES):
                outs[first + d][:, cols] = result[d * rows : (d + 1) * rows]


def attend_chunk(matching, firsts, rests, paired, queries, asked_columns, head_size):
    count, rows = len(queries), queries[0].shape[0]
    block, width = paired.shape[2:]
    scale = math.log2(math.e) / math.sqrt(head_size)
    flops = 4 * count * rows * (1 + ROUNDS) * block * width
    shape = jax.ShapeDtypeStruct((rows, width), paired.dtype)
    return local_call(
        lambda *refs: attention_kernel(head_size, scale, *asked_columns, *refs),
        [shape] * count,
        [matching],
        [*firsts, *rests, paired, *queries],
        grant=24,
        scratch_shapes=[pltpu.VMEM(((1 + ROUNDS) * block, width), paired.dtype)] * 2
        + [
            pltpu.VMEM((count * rows, width), paired.dtype),
            pltpu.VMEM((2, TILE_PIECES * rows, (1 + ROUNDS) * block), jnp.float32),
        ],
        cost_estimate=pl.CostEstimate(
            flops=flops, bytes_accessed=12 * block * width * 2, transcendentals=flops // (4 * head_size)
        ),
    )


def join(pieces, starts, total):
    chunks, count = len(pieces), len(pieces[0])
    share = total // count

    def kernel(*refs):
        for d in range(count):
            for j in range(chunks):
                cols = columns_of(d, share, starts[j], pieces[j][d].shape[1])
                refs[chunks * count][:, cols] = refs[j * count + d][...]

    shape = jax.ShapeDtypeStruct((pieces[0][0].shape[0], total), pieces[0][0].dtype)
    return local_call(kernel, shape, [], [p for per in pieces for p in per])


def cube(query_tokens, key_tokens, value_tokens, matching):
    seq_count, head_count = lax.axis_size("seq"), lax.axis_size("head")
    _, total = key_tokens.shape
    share = total // head_count
    widths = [share // 6 * size for size in SIXTHS]
    starts = [sum(widths[:j]) for j in range(len(SIXTHS))]
    chunks = range(len(SIXTHS))

    def over_seq(x, bits):
        return lax.ppermute(x, "seq", [(i, i ^ bits) for i in range(seq_count)])

    def exchange(x, bits):
        return lax.ppermute(x, "head", [(i, i ^ bits) for i in range(head_count)])

    ways = range(head_count)

    def spread(own):
        near, far = over_seq(own, 2), over_seq(own, 4)
        keys, values = halves(near, far)
        return own, near, far, over_seq(keys, 4), over_seq(values, 2)

    first, own_queries = split_own(key_tokens, value_tokens, query_tokens, share)
    firsts = spread(first)
    tokens = {"k": key_tokens, "v": value_tokens, "q": query_tokens}
    found = {}
    for stage in STAGES:
        which = [(name[0], int(name[1:])) for name in stage]
        parts = [(tokens[kind], share, starts[j], widths[j]) for kind, j in which]
        pieces = split(ways[1:], parts)
        pieces = [exchange(p, d) for d, p in zip(ways[1:], pieces)]
        column = 0
        for kind, j in which:
            found[kind, j] = pieces, column
            column += widths[j]

    results = []
    for j in chunks:
        pieces, column = found["k", j]
        own = pack(pieces, (column, found["v", j][1]), widths[j])
        rests = spread(own)
        picked = pick(matching, firsts, rests, starts[j])
        paired = over_seq(picked, 1)
        pieces, column = found["q", j]
        queries = [own_queries, *pieces]
        columns = [starts[j]] + [column] * len(pieces)
        halfway = head_count // 2 if j == len(SIXTHS) - 1 else 0
        outs = []
        for part in (slice(halfway, None), slice(0, halfway)):
            if queries[part]:
                outs = [
                    *attend_chunk(
                        matching,
                        firsts,
                        rests,
                        paired,
                        queries[part],
                        (starts[j], columns[part]),
                        HEAD_DIM,
                    ),
                    *outs,
                ]
        results.append([outs[0]] + [exchange(outs[d], d) for d in ways[1:]])
    return join(results, starts, total)


def fits_cube(seq_count, head_count, heads):
    power = head_count & (head_count - 1) == 0
    return seq_count == 2**3 and power and heads % (head_count * 6) == 0


def per_device(query_tokens, key_tokens, value_tokens, matching):
    seq_count, head_count = lax.axis_size("seq"), lax.axis_size("head")
    if fits_cube(seq_count, head_count, key_tokens.shape[1] // HEAD_DIM):
        return cube(query_tokens, key_tokens, value_tokens, matching)
    return routed(query_tokens, key_tokens, value_tokens, matching)


def solution(mesh):
    return jax.shard_map(
        per_device,
        mesh=mesh,
        in_specs=(
            P(("seq", "head"), None),
            P(("seq", "head"), None),
            P(("seq", "head"), None),
            P(),
        ),
        out_specs=P(("seq", "head"), None),
        check_vma=False,
    )
```
